32 devices in a mesh: comp: 2 (over y), tile: 16 (over z, x, core).
Axes of the slice: x: 2, y: 2, z: 4, core: 2. Of those that a mesh axis runs over, the one named last changes fastest.
Arguments:
- model_state: float32 [2, 4, 12, 512, 1024], P('comp', None, None, 'tile'), may hold values from -6 to 6
- sea_mask: int32 [2, 512, 1024], P('comp', 'tile'), may hold values 0 or 1
- diffusion: float32 [2, 4], P('comp'), may hold values from 0.02 to 0.24
- vertical_mix: float32 [2, 4, 12, 12], P('comp'), may hold values from -0.4 to 0.4
- export_mix: float32 [2, 16, 4], P('comp'), may hold values from -3 to 3
- import_mix: float32 [2, 4, 16], P('comp'), may hold values from -1.5 to 1.5
- pair_source: int32 [2, 3072], P('comp', 'tile'), may hold values from 0 to 255
- pair_tile: int32 [2, 3072], P('comp', 'tile'), may hold values from 0 to 15, as said below
- pair_block: int32 [2, 3072], P('comp', 'tile'), may hold values from 0 to 255
- pair_count: int32 [2, 16], P('comp', 'tile'), may hold values from 144 to 192, as said below
- pair_weight: bfloat16 [2, 3072, 128, 128], P('comp', 'tile'), may hold values from -0.5 to 0.5
Outputs:
- advanced_state: float32 [2, 4, 12, 512, 1024], P('comp', None, None, 'tile')
The draws below stay inside these ranges and needn't reach their ends.
Inputs may be any that keep to these rules, and one draw needn't show every extreme that they name: `pair_count`: slots at or beyond a tile's count are unused; in each component some tile uses all 192. `pair_tile`: among the used slots of one tile at most 24 name one destination tile; in each component one destination tile is named 24 times by the used slots of every tile.
All inputs are finite; a program needn't handle non-finite values. No bound on the sum of `sea_mask` on one device may be relied on, other than what follows from the above.
Results may differ from the reference program's by a relative error of at most 0.0015.
Values may be sent and summed in bfloat16 or wider, within the bound.
A program may use at most 192 MiB of HBM per device.

```python
import math
import jax
import jax.numpy as jnp
from jax import lax

FIELDS = 4
LEVELS = 12
CHANNELS = 16
BLOCK_CELLS = 128
STEP_COUNT = 2
ROW_CELLS = 1024
PAIR_SLOTS = 192
TILE_COUNT = 16
GRID_ROWS = 512
BLOCKS_TILE = 256
CAPACITY = 24
PAIRS_ALL = 3072


def draw_pair_count(key, part):
    live_least = (3 * PAIR_SLOTS + 3) // 4
    counts = jax.random.randint(jax.random.fold_in(key, 11), (2, TILE_COUNT), live_least, PAIR_SLOTS + 1)
    fullest = jax.random.randint(jax.random.fold_in(key, 12), (2, 1), 0, TILE_COUNT)
    return jnp.where(jnp.arange(TILE_COUNT)[None, :] == fullest, PAIR_SLOTS, counts).astype(jnp.int32)


def draw_pair_tile(key, part):
    live_least = (3 * PAIR_SLOTS + 3) // 4
    homes = jax.random.randint(jax.random.fold_in(key, 21), (2,), 0, TILE_COUNT).astype(jnp.int32)
    list_keys = jax.random.split(jax.random.fold_in(key, 22), 2 * TILE_COUNT)
    pool_tiles = jnp.repeat(jnp.arange(TILE_COUNT - 1, dtype=jnp.int32), CAPACITY)

    def one_list(each_key, home):
        first_key, second_key = jax.random.split(each_key)
        others = jax.random.permutation(first_key, pool_tiles)[:PAIR_SLOTS - CAPACITY]
        others = others + (others >= home).astype(jnp.int32)
        listing = jnp.concatenate([jnp.full((CAPACITY,), home, jnp.int32), others])
        head_part = jax.random.permutation(second_key, listing[:live_least])
        return jnp.concatenate([head_part, listing[live_least:]])
    home_each = jnp.repeat(homes, TILE_COUNT)
    all_lists = jax.vmap(one_list)(list_keys, home_each)
    return all_lists.reshape(2, TILE_COUNT * PAIR_SLOTS).astype(jnp.int32)


def place_ends(result, stream_key, low, high):
    longest = result.shape.index(max(result.shape))
    spots = []
    for shift in (0, 1):
        where = [jax.random.randint(jax.random.fold_in(stream_key, axis), (), 0, length) for axis, length in enumerate(result.shape)]
        where[longest] = (where[longest] + shift) % result.shape[longest]
        spots.append(tuple(where))
    return result.at[spots[0]].set(low).at[spots[1]].set(high)


def level_of(key, dims, cuts, smallest, high):
    def one(axis_at, blocks):
        steps = jax.random.uniform(jax.random.fold_in(jax.random.fold_in(key, 6), axis_at), (blocks,), jnp.float32, smallest / len(cuts), high / len(cuts))
        return jnp.repeat(jnp.exp(steps), dims[axis_at] // blocks).reshape((-1,) + (1,) * (len(dims) - axis_at - 1))

    level = one(*cuts[0])
    for cut in cuts[1:]:
        level = level * one(*cut)
    return level


def noise(own_key, extent, scale, most, cuts=(), kind=jnp.bfloat16):
    drawn = jax.random.normal(own_key, extent, jnp.float32) * scale
    if len(cuts) > 0:
        drawn = level_of(own_key, extent, cuts, -0.22, 0.18) * drawn
    return jnp.clip(drawn, min=-most, max=most).astype(kind)


def setup_inputs(seed: int = 0) -> dict:
    arg_keys = jax.random.split(jax.random.key(seed), 12)
    return {
        "model_state": noise(arg_keys[0], (2, FIELDS, LEVELS, GRID_ROWS, ROW_CELLS), 1.0, 6.0, ((0, 2), (3, 16)), jnp.float32),
        "sea_mask": place_ends((jax.random.randint(arg_keys[1], (2, GRID_ROWS, ROW_CELLS), 0, 10) < 7).astype(jnp.int32), jax.random.fold_in(arg_keys[1], 1), 0, 1),
        "diffusion": jnp.clip(jnp.exp(math.log(0.24) - 2.4849066 * jax.random.uniform(arg_keys[2], (2, FIELDS), jnp.float32) ** level_of(arg_keys[2], (2, FIELDS), ((0, 2),), -0.2, 0.2)), 0.02, 0.24),
        "vertical_mix": noise(arg_keys[3], (2, FIELDS, LEVELS, LEVELS), 0.08, 0.4, ((0, 2),), jnp.float32),
        "export_mix": noise(arg_keys[4], (2, CHANNELS, FIELDS), FIELDS ** -0.5, 3.0, ((0, 2),), jnp.float32),
        "import_mix": noise(arg_keys[5], (2, FIELDS, CHANNELS), CHANNELS ** -0.5, 1.5, ((0, 2),), jnp.float32),
        "pair_source": place_ends(jax.random.randint(arg_keys[6], (2, PAIRS_ALL), 0, BLOCKS_TILE), jax.random.fold_in(arg_keys[6], 1), 0, BLOCKS_TILE - 1).astype(jnp.int32),
        "pair_tile": draw_pair_tile(jax.random.fold_in(arg_keys[11], 71), 0),
        "pair_block": place_ends(jax.random.randint(arg_keys[8], (2, PAIRS_ALL), 0, BLOCKS_TILE), jax.random.fold_in(arg_keys[8], 1), 0, BLOCKS_TILE - 1).astype(jnp.int32),
        "pair_count": draw_pair_count(jax.random.fold_in(arg_keys[11], 71), 0),
        "pair_weight": noise(arg_keys[10], (2, PAIRS_ALL, BLOCK_CELLS, BLOCK_CELLS), BLOCK_CELLS ** -0.5, 0.5, ((0, 2), (1, 16))),
    }


HIGHEST = lax.Precision.HIGHEST


def advance(current, rate_field, mixing_field):
    padded = jnp.pad(current, ((0, 0), (1, 1), (0, 0)))
    laplace = padded[:, 2:, :] + padded[:, :-2, :] + jnp.roll(current, 1, axis=2) + jnp.roll(current, -1, axis=2) - 4.0 * current
    vertical = jnp.einsum("lm,myx->lyx", mixing_field, current, precision=HIGHEST)
    return current + rate_field * laplace + vertical


def stepped_fields(state_part, rates, mixing):
    def one_field(operands):
        current, rate_field, mixing_field = operands
        for sweep in range(STEP_COUNT):
            current = advance(current, rate_field, mixing_field)
        return current

    return lax.map(one_field, (state_part, rates, mixing))


def remap(exports, pair_source, pair_tile, pair_block, pair_count, pair_weight):
    blocks = exports.reshape(CHANNELS, TILE_COUNT * BLOCKS_TILE, BLOCK_CELLS)
    starts = jnp.arange(TILE_COUNT, dtype=jnp.int32)[:, None] * BLOCKS_TILE
    sources = (starts + pair_source.reshape(TILE_COUNT, PAIR_SLOTS)).astype(jnp.int32)
    targets = (pair_tile.reshape(TILE_COUNT, PAIR_SLOTS) * BLOCKS_TILE + pair_block.reshape(TILE_COUNT, PAIR_SLOTS)).astype(jnp.int32)
    is_live = jnp.arange(PAIR_SLOTS, dtype=jnp.int32)[None, :] < pair_count[:, None]
    weights = pair_weight.reshape(TILE_COUNT, PAIR_SLOTS, BLOCK_CELLS, BLOCK_CELLS)

    def tile_terms(operands):
        tile_sources, tile_weights, tile_live = operands
        picked = blocks[:, tile_sources].astype(jnp.float32)
        contrib = jnp.einsum("kpb,pbc->pkc", picked, tile_weights.astype(jnp.float32), precision=HIGHEST)
        contrib = lax.optimization_barrier(contrib.astype(jnp.bfloat16))
        contrib = contrib.astype(jnp.float32)
        return jnp.where(tile_live[:, None, None], contrib, jnp.zeros((), jnp.float32))

    terms = lax.map(tile_terms, (sources, weights, is_live))
    imports = jnp.zeros((TILE_COUNT * BLOCKS_TILE, CHANNELS, BLOCK_CELLS), jnp.float32)
    imports = imports.at[targets.reshape(-1)].add(terms.reshape(-1, CHANNELS, BLOCK_CELLS))
    return imports.transpose(1, 0, 2).reshape(CHANNELS, GRID_ROWS, ROW_CELLS)


def reference(model_state, sea_mask, diffusion, vertical_mix, export_mix, import_mix, pair_source, pair_tile, pair_block, pair_count, pair_weight):
    imports = []
    for component in range(2):
        exports = jnp.einsum("kf,fyx->kyx", export_mix[component], model_state[component, :, 0], precision=HIGHEST).astype(jnp.bfloat16)
        imports.append(remap(exports, pair_source[component], pair_tile[component], pair_block[component], pair_count[component], pair_weight[component]))
    results = []
    for component in range(2):
        stepped = stepped_fields(model_state[component], diffusion[component], vertical_mix[component])
        forcing = jnp.einsum("fk,kyx->fyx", import_mix[component], imports[1 - component], precision=HIGHEST)
        forcing = forcing * sea_mask[component].astype(jnp.float32)
        results.append(stepped.at[:, 0].add(forcing))
    return jnp.stack(results)
```

```python
import functools

import jax
import jax.numpy as jnp
from jax import lax
from jax.experimental import pallas as pl
from jax.experimental.pallas import tpu as pltpu
from jax.sharding import PartitionSpec as P

CELLS = 128
STEPS = 2
GROUP = 16
PAD = 8
LANE = 32
HIGHEST = lax.Precision.HIGHEST
MESH = pl.DeviceIdType.MESH
F32 = jnp.float32
BF16 = jnp.bfloat16


def iota(shape, dim):
    return lax.broadcasted_iota(jnp.int32, shape, dim)


def onehot(cond, dtype=F32):
    return jnp.where(cond, 1.0, 0.0).astype(dtype)


def exact_dot(a, b):
    return jnp.dot(a, b, precision=HIGHEST, preferred_element_type=F32)


def kron(mix_ref, f, fields, levels):
    mix = jnp.zeros((levels, levels), F32)
    for g in range(fields):
        mix = mix + jnp.where(f == g, 1.0, 0.0) * mix_ref[0, :, g, :]
    side = levels * GROUP
    left = onehot(iota((side, levels), 0) // GROUP == iota((side, levels), 1), BF16)
    right = onehot(iota((levels, side), 0) == iota((levels, side), 1) // GROUP, BF16)
    same = iota((side, side), 0) % GROUP == iota((side, side), 1) % GROUP
    high = mix.astype(BF16)
    low = (mix - high.astype(F32)).astype(BF16)

    def spread(part):
        part = jnp.dot(left, part, preferred_element_type=F32).astype(BF16)
        part = jnp.dot(part, right, preferred_element_type=F32)
        return jnp.where(same, part, 0.0).astype(BF16)

    return spread(high), spread(low)


def column(high, low, v, passes):
    levels, rows, width = v.shape
    vh = v.astype(BF16)
    vh2 = vh.reshape(levels * rows, width)
    out = jnp.dot(high, vh2, preferred_element_type=F32)
    out = out + jnp.dot(low, vh2, preferred_element_type=F32)
    if passes > 2:
        vl = (v - vh.astype(F32)).astype(BF16).reshape(levels * rows, width)
        out = out + jnp.dot(high, vl, preferred_element_type=F32)
    return out


def around(v):
    rows, width = v.shape
    return (
        pltpu.roll(v, 1, 0) + pltpu.roll(v, rows - 1, 0) + pltpu.roll(v, 1, 1) + pltpu.roll(v, width - 1, 1)
    )


def send_kernel(
    cap,
    chunk,
    lead,
    src_ref,
    count_ref,
    diff_ref,
    tile_ref,
    block_ref,
    state_ref,
    first_ref,
    last_ref,
    mix_ref,
    imix_ref,
    vmix_ref,
    w_ref,
    x_ref,
    recv_ref,
    ids_ref,
    out_ref,
    exports,
    contribs,
    mixed,
    payload,
    id_rows,
    im_send,
    im_recv,
    edges,
    halo,
    meta,
    ext,
    vert,
    pay_send_sem,
    pay_recv_sem,
    id_send_sem,
    id_recv_sem,
    small_send_sem,
    small_recv_sem,
):
    step = pl.program_id(0)
    me_c = lax.axis_index("comp")
    me_t = lax.axis_index("tile")
    n = recv_ref.shape[0]
    other = 1 - me_c
    above = lax.rem(me_t + 1, n)
    below = lax.rem(me_t + n - 1, n)
    fields, tile_rows, width = state_ref.shape[1], state_ref.shape[3], state_ref.shape[4]
    channels = mix_ref.shape[2]
    levels = x_ref.shape[2]
    xblocks = width // CELLS
    per_step = w_ref.shape[1]

    def halo_copies():
        return (
            pltpu.make_async_remote_copy(
                src_ref=edges.at[0],
                dst_ref=halo.at[1],
                send_sem=small_send_sem.at[0],
                recv_sem=small_recv_sem.at[0],
                device_id=(me_c, below),
                device_id_type=MESH,
            ),
            pltpu.make_async_remote_copy(
                src_ref=edges.at[1],
                dst_ref=halo.at[0],
                send_sem=small_send_sem.at[1],
                recv_sem=small_recv_sem.at[1],
                device_id=(me_c, above),
                device_id_type=MESH,
            ),
        )

    def mix_copy():
        return pltpu.make_async_remote_copy(
            src_ref=im_send,
            dst_ref=im_recv,
            send_sem=small_send_sem.at[2],
            recv_sem=small_recv_sem.at[2],
            device_id=(other, me_t),
            device_id_type=MESH,
        )

    def block_copies(to, source_slot):
        return (
            pltpu.make_async_remote_copy(
                src_ref=id_rows.at[to],
                dst_ref=ids_ref.at[source_slot],
                send_sem=id_send_sem.at[to],
                recv_sem=id_recv_sem.at[source_slot],
                device_id=(other, to),
                device_id_type=MESH,
            ),
            pltpu.make_async_remote_copy(
                src_ref=payload.at[to],
                dst_ref=recv_ref.at[source_slot],
                send_sem=pay_send_sem.at[to],
                recv_sem=pay_recv_sem.at[source_slot],
                device_id=(other, to),
                device_id_type=MESH,
            ),
        )

    @pl.when(step == 0)
    def _():
        barrier = pltpu.get_barrier_semaphore()

        def greet(t, carry):
            pl.semaphore_signal(barrier, inc=1, device_id=(other, t), device_id_type=MESH)
            return carry

        lax.fori_loop(0, n, greet, 0)
        pl.semaphore_signal(barrier, inc=1, device_id=(me_c, above), device_id_type=MESH)
        pl.semaphore_signal(barrier, inc=1, device_id=(me_c, below), device_id_type=MESH)
        im_send[...] = jnp.zeros_like(im_send)
        im_send[0:fields, 0:channels] = imix_ref[0]
        for f in range(fields):
            for r in range(2):
                edges[0, f, r] = first_ref[0, f, :, r, :].astype(BF16)
                edges[1, f, r] = last_ref[0, f, :, 6 + r, :].astype(BF16)
        pl.semaphore_wait(barrier, n + 2)
        for copy in halo_copies():
            copy.start()
        mix_copy().start()
        sub = 8
        rows = sub * channels
        cols = sub * fields
        left = onehot(iota((rows, channels), 0) % channels == iota((rows, channels), 1))
        right = onehot(iota((fields, cols), 0) == iota((fields, cols), 1) // sub)
        by_channel = lax.dot_general(
            left,
            mix_ref[0],
            (((1,), (1,)), ((), ())),
            precision=HIGHEST,
            preferred_element_type=F32,
        )
        spread = exact_dot(by_channel, right)
        spread = jnp.where(
            iota((rows, cols), 0) // channels == iota((rows, cols), 1) % sub, spread, 0.0
        )
        for g in range(tile_rows // sub):
            s = state_ref[0, :, 0, g * sub : (g + 1) * sub, :].reshape(cols, width)
            e = exact_dot(spread, s).astype(BF16)
            for y in range(sub):
                for xb in range(xblocks):
                    exports[(g * sub + y) * xblocks + xb] = e[
                        y * channels : (y + 1) * channels, xb * CELLS : (xb + 1) * CELLS
                    ]
        ext[...] = jnp.zeros_like(ext)

    @pl.when(step < lead)
    def _():
        for p in range(per_step):
            picked = exports[src_ref[0, step * per_step + p]]
            c = jnp.dot(picked, w_ref[0, p], preferred_element_type=F32)
            at = (p % GROUP) * channels
            contribs[step * (per_step // GROUP) + p // GROUP, at : at + channels, :] = c.astype(BF16)

    @pl.when(step == lead - 1)
    def _():
        mix_copy().wait()
        rows = fields * GROUP
        cols = GROUP * channels
        left = onehot(iota((rows, 8), 0) // GROUP == iota((rows, 8), 1))
        right = onehot(iota((CELLS, cols), 0) == iota((CELLS, cols), 1) % channels)
        blend = exact_dot(exact_dot(left, im_recv[...]), right)
        blend = jnp.where(iota((rows, cols), 0) % GROUP == iota((rows, cols), 1) // channels, blend, 0.0)
        high = blend.astype(BF16)
        low = (blend - high.astype(F32)).astype(BF16)
        slots = contribs.shape[0] * GROUP
        wide = mixed.shape[0]
        mixed[slots:, :] = jnp.zeros((wide - slots, fields * CELLS), BF16)
        for g in range(contribs.shape[0]):
            cb = contribs[g]
            m = jnp.dot(high, cb, preferred_element_type=F32) + jnp.dot(
                low, cb, preferred_element_type=F32
            )
            m = m.astype(BF16)
            for f in range(fields):
                mixed[g * GROUP : (g + 1) * GROUP, f * CELLS : (f + 1) * CELLS] = m[
                    f * GROUP : (f + 1) * GROUP, :
                ]
        meta[...] = jnp.zeros_like(meta)
        meta[0:1, 0:slots] = tile_ref[...]
        meta[1:2, 0:slots] = block_ref[...]
        lane = iota((1, wide), 1)
        live = lane < count_ref[0, 0]
        tiles = jnp.where(live, meta[0:1, :], -1)
        square_row = iota((wide, wide), 0)
        square_col = iota((wide, wide), 1)
        tile_square = jnp.broadcast_to(tiles, (wide, wide))
        tile_col = jnp.sum(
            jnp.where(square_row == square_col, tile_square, 0), axis=1, keepdims=True
        )
        same = (tile_col == tile_square) & (square_row < square_col)
        rank = jnp.sum(jnp.where(same, 1, 0), axis=0, keepdims=True)
        slot = jnp.where(live, tiles * chunk + rank, -1)
        dest = jnp.where(
            (iota((n, wide), 0) == tiles) & live,
            jnp.broadcast_to(meta[1:2, :] + 1, (n, wide)),
            0,
        )
        base = lax.rem(me_t, CELLS // LANE) * LANE
        spot = onehot(iota((CELLS, wide), 0) == rank + base, BF16)
        index_rows = lax.dot_general(
            dest.astype(F32).astype(BF16), spot, (((1,), (1,)), ((), ())), preferred_element_type=F32
        )
        for t in range(n):
            id_rows[t] = jnp.broadcast_to(index_rows[t : t + 1, :], (8, CELLS)).astype(BF16)
        for d in range(0, n, 8):
            place = onehot(iota((8 * chunk, wide), 0) + d * chunk == slot, BF16)
            block = jnp.dot(place, mixed[...], preferred_element_type=F32)
            for j in range(8):
                payload[d + j] = block[j * chunk : (j + 1) * chunk, :].astype(BF16)

        def send(k, carry):
            for copy in block_copies(lax.rem(me_t + k, n), me_t):
                copy.start()
            return carry

        lax.fori_loop(0, n, send, 0)
        for copy in halo_copies():
            copy.wait()

    @pl.when(step >= lead)
    def _():
        f = step - lead
        low_on = jnp.where(me_t > 0, 1.0, 0.0).astype(F32)
        high_on = jnp.where(me_t < n - 1, 1.0, 0.0).astype(F32)
        d = diff_ref[0, f]
        high, low = kron(vmix_ref, f, fields, levels)
        ext[:, PAD : PAD + tile_rows, :] = x_ref[0, 0]
        for r in range(2):
            ext[:, PAD - 2 + r : PAD - 1 + r, :] = (halo[0, f, r].astype(F32) * low_on)[:, None, :]
            at = PAD + tile_rows + r
            ext[:, at : at + 1, :] = (halo[1, f, r].astype(F32) * high_on)[:, None, :]
        total = tile_rows + 2 * PAD
        for g in range(total // GROUP):
            vert[g] = column(high, low, ext[:, g * GROUP : (g + 1) * GROUP, :], 3)
        row = iota((total, 1), 0)
        keep = jnp.where(row < PAD, low_on, jnp.where(row >= PAD + tile_rows, high_on, 1.0))
        for lev in range(levels):
            v = ext[lev]
            lift = vert[:, lev * GROUP : (lev + 1) * GROUP, :].reshape(total, width)
            out_ref[0, lev] = (v * (1.0 - 4.0 * d) + around(v) * d + lift) * keep

    @pl.when(step == pl.num_programs(0) - 1)
    def _():
        def finish(t, carry):
            for copy in block_copies(t, t):
                copy.wait()
            return carry

        lax.fori_loop(0, n, finish, 0)


def step_kernel(
    diff_ref,
    v_ref,
    vmix_ref,
    recv_ref,
    ids_ref,
    mask_ref,
    out_ref,
    vert,
    hits,
    packed,
):
    f = pl.program_id(0)
    n, chunk = recv_ref.shape[0], recv_ref.shape[1]
    levels, total, width = v_ref.shape[1], v_ref.shape[2], v_ref.shape[3]
    fields = vmix_ref.shape[2]
    rows = total - 2 * PAD
    xblocks = width // CELLS
    per_group = CELLS // LANE

    @pl.when(f == 0)
    def _():
        for g in range(n // per_group):
            ids = jnp.zeros((8, CELLS), F32)
            for j in range(per_group):
                ids = ids + ids_ref[g * per_group + j].astype(F32)
            ids = ids[0:1, :].astype(jnp.int32) - 1
            spot = jnp.where(ids >= 0, (ids % xblocks) * rows + ids // xblocks, -1)
            hits[:, g * CELLS : (g + 1) * CELLS] = onehot(
                iota((rows * xblocks, CELLS), 0) == spot, BF16
            )
        for t in range(n):
            packed[t, 0:chunk, :] = recv_ref[t]
            packed[t, chunk:, :] = jnp.zeros((LANE - chunk, packed.shape[2]), BF16)

    d = diff_ref[0, f]
    high, low = kron(vmix_ref, f, fields, levels)
    for g in range(rows // GROUP):
        at = PAD + g * GROUP
        vert[g] = column(high, low, v_ref[0, :, at : at + GROUP, :], 2)
    for lev in range(levels):
        v = v_ref[0, lev]
        lift = vert[:, lev * GROUP : (lev + 1) * GROUP, :].reshape(rows, width)
        near = v * (1.0 - 4.0 * d) + around(v) * d
        out_ref[0, 0, lev] = near[PAD : PAD + rows, :] + lift

    part = packed[:, :, pl.ds(pl.multiple_of(f * CELLS, CELLS), CELLS)].reshape(n * LANE, CELLS)
    forcing = jnp.dot(hits[...], part, preferred_element_type=F32)
    for xb in range(xblocks):
        cols = slice(xb * CELLS, (xb + 1) * CELLS)
        out_ref[0, 0, 0, :, cols] += forcing[xb * rows : (xb + 1) * rows, :] * mask_ref[
            0, :, cols
        ].astype(F32)


def local(
    model_state,
    sea_mask,
    diffusion,
    vertical_mix,
    export_mix,
    import_mix,
    pair_source,
    pair_tile,
    pair_block,
    pair_count,
    pair_weight,
):
    _, fields, levels, rows, width = model_state.shape
    channels = export_mix.shape[1]
    n = lax.axis_size("tile")
    slots = pair_source.shape[1]
    cap = (2 * slots + n - 1) // n
    chunk = -(-cap // 8) * 8
    wide = -(-slots // 128) * 128
    blocks = rows * width // CELLS
    total = rows + 2 * PAD
    lead = 4
    per_step = slots // lead
    last_rows = rows // 8 - 1

    vmix = vertical_mix.transpose(0, 2, 1, 3)
    smem = pl.BlockSpec(memory_space=pltpu.SMEM)
    hbm = pl.BlockSpec(memory_space=pl.ANY)

    def whole(shape):
        return pl.BlockSpec(shape, lambda i: (0,) * len(shape))

    def late(i):
        return lax.div(i, lead) * (i - lead)

    def early(i):
        return i + lax.div(i, lead) * (lead - 1 - i)

    received, ids, stepped = pl.pallas_call(
        functools.partial(send_kernel, cap, chunk, lead),
        grid=(lead + fields,),
        out_shape=(
            jax.ShapeDtypeStruct((n, chunk, fields * CELLS), BF16),
            jax.ShapeDtypeStruct((n, 8, CELLS), BF16),
            jax.ShapeDtypeStruct((fields, levels, total, width), F32),
        ),
        in_specs=[
            smem,
            smem,
            smem,
            whole((1, slots)),
            whole((1, slots)),
            whole((1, fields, 1, rows, width)),
            whole((1, fields, levels, 8, width)),
            pl.BlockSpec((1, fields, levels, 8, width), lambda i: (0, 0, 0, last_rows, 0)),
            whole((1, fields, channels)),
            whole((1, fields, channels)),
            whole((1, levels, fields, levels)),
            pl.BlockSpec((1, per_step, CELLS, CELLS), lambda i: (0, early(i), 0, 0)),
            pl.BlockSpec((1, 1, levels, rows, width), lambda i: (0, late(i), 0, 0, 0)),
        ],
        out_specs=(
            hbm,
            hbm,
            pl.BlockSpec((1, levels, total, width), lambda i: (late(i), 0, 0, 0)),
        ),
        scratch_shapes=[
            pltpu.VMEM((blocks, channels, CELLS), BF16),
            pltpu.VMEM((slots // GROUP, GROUP * channels, CELLS), BF16),
            pltpu.VMEM((wide, fields * CELLS), BF16),
            pltpu.VMEM((n, chunk, fields * CELLS), BF16),
            pltpu.VMEM((n, 8, CELLS), BF16),
            pltpu.VMEM((8, CELLS), F32),
            pltpu.VMEM((8, CELLS), F32),
            pltpu.VMEM((2, fields, 2, levels, width), BF16),
            pltpu.VMEM((2, fields, 2, levels, width), BF16),
            pltpu.VMEM((8, wide), jnp.int32),
            pltpu.VMEM((levels, total, width), F32),
            pltpu.VMEM((total // GROUP, levels * GROUP, width), F32),
            pltpu.SemaphoreType.DMA((n,)),
            pltpu.SemaphoreType.DMA((n,)),
            pltpu.SemaphoreType.DMA((n,)),
            pltpu.SemaphoreType.DMA((n,)),
            pltpu.SemaphoreType.DMA((3,)),
            pltpu.SemaphoreType.DMA((3,)),
        ],
        compiler_params=pltpu.CompilerParams(
            collective_id=0, has_side_effects=True, vmem_limit_bytes=58 << 20
        ),
    )(
        pair_source,
        pair_count,
        diffusion,
        pair_tile,
        pair_block,
        model_state,
        model_state,
        model_state,
        export_mix.transpose(0, 2, 1),
        import_mix,
        vmix,
        pair_weight,
        model_state,
    )

    return pl.pallas_call(
        step_kernel,
        grid=(fields,),
        out_shape=jax.ShapeDtypeStruct(model_state.shape, F32),
        in_specs=[
            smem,
            pl.BlockSpec((1, levels, total, width), lambda i: (i, 0, 0, 0)),
            whole((1, levels, fields, levels)),
            whole((n, chunk, fields * CELLS)),
            whole((n, 8, CELLS)),
            whole((1, rows, width)),
        ],
        out_specs=pl.BlockSpec((1, 1, levels, rows, width), lambda i: (0, i, 0, 0, 0)),
        scratch_shapes=[
            pltpu.VMEM((rows // GROUP, levels * GROUP, width), F32),
            pltpu.VMEM((blocks, n * LANE), BF16),
            pltpu.VMEM((n, LANE, fields * CELLS), BF16),
        ],
        compiler_params=pltpu.CompilerParams(vmem_limit_bytes=48 << 20),
    )(diffusion, stepped, vmix, received, ids, sea_mask)


def solution(mesh):
    return jax.shard_map(
        local,
        mesh=mesh,
        in_specs=(
            P("comp", None, None, "tile", None),
            P("comp", "tile", None),
            P("comp", None),
            P("comp", None, None, None),
            P("comp", None, None),
            P("comp", None, None),
            P("comp", "tile"),
            P("comp", "tile"),
            P("comp", "tile"),
            P("comp", "tile"),
            P("comp", "tile", None, None),
        ),
        out_specs=P("comp", None, None, "tile", None),
        check_vma=False,
    )
```

```python
import functools

import jax
import jax.numpy as jnp
from jax import lax
from jax.experimental import pallas as pl
from jax.experimental.pallas import tpu as pltpu
from jax.sharding import PartitionSpec as P

CELLS = 128
STEPS = 2
GROUP = 16
PAD = 8
LANE = 32
HIGHEST = lax.Precision.HIGHEST
MESH = pl.DeviceIdType.MESH
F32 = jnp.float32
BF16 = jnp.bfloat16


def iota(shape, dim):
    return lax.broadcasted_iota(jnp.int32, shape, dim)


def onehot(cond, dtype=F32):
    return jnp.where(cond, 1.0, 0.0).astype(dtype)


def exact_dot(a, b):
    return jnp.dot(a, b, precision=HIGHEST, preferred_element_type=F32)


def kron(mix_ref, f, fields, levels):
    mix = jnp.zeros((levels, levels), F32)
    for g in range(fields):
        mix = mix + jnp.where(f == g, 1.0, 0.0) * mix_ref[0, :, g, :]
    side = levels * GROUP
    left = onehot(iota((side, levels), 0) // GROUP == iota((side, levels), 1), BF16)
    right = onehot(iota((levels, side), 0) == iota((levels, side), 1) // GROUP, BF16)
    same = iota((side, side), 0) % GROUP == iota((side, side), 1) % GROUP
    high = mix.astype(BF16)
    low = (mix - high.astype(F32)).astype(BF16)

    def spread(part):
        part = jnp.dot(left, part, preferred_element_type=F32).astype(BF16)
        part = jnp.dot(part, right, preferred_element_type=F32)
        return jnp.where(same, part, 0.0).astype(BF16)

    return spread(high), spread(low)


def column(high, low, v, passes):
    levels, rows, width = v.shape
    vh = v.astype(BF16)
    vh2 = vh.reshape(levels * rows, width)
    out = jnp.dot(high, vh2, preferred_element_type=F32)
    out = out + jnp.dot(low, vh2, preferred_element_type=F32)
    if passes > 2:
        vl = (v - vh.astype(F32)).astype(BF16).reshape(levels * rows, width)
        out = out + jnp.dot(high, vl, preferred_element_type=F32)
    return out


def around(v):
    rows, width = v.shape
    return (
        pltpu.roll(v, 1, 0) + pltpu.roll(v, rows - 1, 0) + pltpu.roll(v, 1, 1) + pltpu.roll(v, width - 1, 1)
    )


def send_kernel(
    cap,
    chunk,
    lead,
    src_ref,
    count_ref,
    diff_ref,
    tile_ref,
    block_ref,
    state_ref,
    first_ref,
    last_ref,
    mix_ref,
    imix_ref,
    vmix_ref,
    w_ref,
    x_ref,
    recv_ref,
    ids_ref,
    out_ref,
    exports,
    contribs,
    mixed,
    payload,
    id_rows,
    im_send,
    im_recv,
    edges,
    halo,
    meta,
    ext,
    vert,
    pay_send_sem,
    pay_recv_sem,
    id_send_sem,
    id_recv_sem,
    small_send_sem,
    small_recv_sem,
):
    step = pl.program_id(0)
    me_c = lax.axis_index("comp")
    me_t = lax.axis_index("tile")
    n = recv_ref.shape[0]
    other = 1 - me_c
    above = lax.rem(me_t + 1, n)
    below = lax.rem(me_t + n - 1, n)
    fields, tile_rows, width = state_ref.shape[1], state_ref.shape[3], state_ref.shape[4]
    channels = mix_ref.shape[2]
    levels = x_ref.shape[2]
    xblocks = width // CELLS
    per_step = w_ref.shape[1]

    def halo_copies():
        return (
            pltpu.make_async_remote_copy(
                src_ref=edges.at[0],
                dst_ref=halo.at[1],
                send_sem=small_send_sem.at[0],
                recv_sem=small_recv_sem.at[0],
                device_id=(me_c, below),
                device_id_type=MESH,
            ),
            pltpu.make_async_remote_copy(
                src_ref=edges.at[1],
                dst_ref=halo.at[0],
                send_sem=small_send_sem.at[1],
                recv_sem=small_recv_sem.at[1],
                device_id=(me_c, above),
                device_id_type=MESH,
            ),
        )

    def mix_copy():
        return pltpu.make_async_remote_copy(
            src_ref=im_send,
            dst_ref=im_recv,
            send_sem=small_send_sem.at[2],
            recv_sem=small_recv_sem.at[2],
            device_id=(other, me_t),
            device_id_type=MESH,
        )

    def block_copies(to, source_slot):
        return (
            pltpu.make_async_remote_copy(
                src_ref=id_rows.at[to],
                dst_ref=ids_ref.at[source_slot],
                send_sem=id_send_sem.at[to],
                recv_sem=id_recv_sem.at[source_slot],
                device_id=(other, to),
                device_id_type=MESH,
            ),
            pltpu.make_async_remote_copy(
                src_ref=payload.at[to],
                dst_ref=recv_ref.at[source_slot],
                send_sem=pay_send_sem.at[to],
                recv_sem=pay_recv_sem.at[source_slot],
                device_id=(other, to),
                device_id_type=MESH,
            ),
        )

    @pl.when(step == 0)
    def _():
        @pl.when(me_t == 0)
        def _():
            halo[0] = jnp.zeros(halo.shape[1:], BF16)

        @pl.when(me_t == n - 1)
        def _():
            halo[1] = jnp.zeros(halo.shape[1:], BF16)

        barrier = pltpu.get_barrier_semaphore()

        def greet(t, carry):
            pl.semaphore_signal(barrier, inc=1, device_id=(other, t), device_id_type=MESH)
            return carry

        lax.fori_loop(0, n, greet, 0)
        pl.semaphore_signal(barrier, inc=1, device_id=(me_c, above), device_id_type=MESH)
        pl.semaphore_signal(barrier, inc=1, device_id=(me_c, below), device_id_type=MESH)
        im_send[...] = jnp.zeros_like(im_send)
        im_send[0:fields, 0:channels] = imix_ref[0]
        for f in range(fields):
            for r in range(2):
                edges[0, f, r] = first_ref[0, f, :, r, :].astype(BF16)
                edges[1, f, r] = last_ref[0, f, :, 6 + r, :].astype(BF16)
        pl.semaphore_wait(barrier, n + 2)
        down, up = halo_copies()

        @pl.when(me_t > 0)
        def _():
            down.start()

        @pl.when(me_t < n - 1)
        def _():
            up.start()

        mix_copy().start()
        sub = 8
        rows = sub * channels
        cols = sub * fields
        left = onehot(iota((rows, channels), 0) % channels == iota((rows, channels), 1))
        right = onehot(iota((fields, cols), 0) == iota((fields, cols), 1) // sub)
        by_channel = lax.dot_general(
            left,
            mix_ref[0],
            (((1,), (1,)), ((), ())),
            precision=HIGHEST,
            preferred_element_type=F32,
        )
        spread = exact_dot(by_channel, right)
        spread = jnp.where(
            iota((rows, cols), 0) // channels == iota((rows, cols), 1) % sub, spread, 0.0
        )
        for g in range(tile_rows // sub):
            s = state_ref[0, :, 0, g * sub : (g + 1) * sub, :].reshape(cols, width)
            e = exact_dot(spread, s).astype(BF16)
            for y in range(sub):
                for xb in range(xblocks):
                    exports[(g * sub + y) * xblocks + xb] = e[
                        y * channels : (y + 1) * channels, xb * CELLS : (xb + 1) * CELLS
                    ]
        ext[...] = jnp.zeros_like(ext)

    @pl.when(step < lead)
    def _():
        for p in range(per_step):
            picked = exports[src_ref[0, step * per_step + p]]
            c = jnp.dot(picked, w_ref[0, p], preferred_element_type=F32)
            at = (p % GROUP) * channels
            contribs[step * (per_step // GROUP) + p // GROUP, at : at + channels, :] = c.astype(BF16)

    @pl.when(step == lead - 1)
    def _():
        mix_copy().wait()
        rows = fields * GROUP
        cols = GROUP * channels
        left = onehot(iota((rows, 8), 0) // GROUP == iota((rows, 8), 1))
        right = onehot(iota((CELLS, cols), 0) == iota((CELLS, cols), 1) % channels)
        blend = exact_dot(exact_dot(left, im_recv[...]), right)
        blend = jnp.where(iota((rows, cols), 0) % GROUP == iota((rows, cols), 1) // channels, blend, 0.0)
        high = blend.astype(BF16)
        low = (blend - high.astype(F32)).astype(BF16)
        slots = contribs.shape[0] * GROUP
        wide = mixed.shape[0]
        mixed[slots:, :] = jnp.zeros((wide - slots, fields * CELLS), BF16)
        for g in range(contribs.shape[0]):
            cb = contribs[g]
            m = jnp.dot(high, cb, preferred_element_type=F32) + jnp.dot(
                low, cb, preferred_element_type=F32
            )
            m = m.astype(BF16)
            for f in range(fields):
                mixed[g * GROUP : (g + 1) * GROUP, f * CELLS : (f + 1) * CELLS] = m[
                    f * GROUP : (f + 1) * GROUP, :
                ]
        meta[...] = jnp.zeros_like(meta)
        meta[0:1, 0:slots] = tile_ref[...]
        meta[1:2, 0:slots] = block_ref[...]
        lane = iota((1, wide), 1)
        live = lane < count_ref[0, 0]
        tiles = jnp.where(live, meta[0:1, :], -1)
        square_row = iota((wide, wide), 0)
        square_col = iota((wide, wide), 1)
        tile_square = jnp.broadcast_to(tiles, (wide, wide))
        tile_col = jnp.sum(
            jnp.where(square_row == square_col, tile_square, 0), axis=1, keepdims=True
        )
        same = (tile_col == tile_square) & (square_row < square_col)
        rank = jnp.sum(jnp.where(same, 1, 0), axis=0, keepdims=True)
        slot = jnp.where(live, tiles * chunk + rank, -1)
        dest = jnp.where(
            (iota((n, wide), 0) == tiles) & live,
            jnp.broadcast_to(meta[1:2, :] + 1, (n, wide)),
            0,
        )
        base = lax.rem(me_t, CELLS // LANE) * LANE
        spot = onehot(iota((CELLS, wide), 0) == rank + base, BF16)
        index_rows = lax.dot_general(
            dest.astype(F32).astype(BF16), spot, (((1,), (1,)), ((), ())), preferred_element_type=F32
        )
        for t in range(n):
            id_rows[t] = jnp.broadcast_to(index_rows[t : t + 1, :], (8, CELLS)).astype(BF16)
        for d in range(0, n, 8):
            place = onehot(iota((8 * chunk, wide), 0) + d * chunk == slot, BF16)
            block = jnp.dot(place, mixed[...], preferred_element_type=F32)
            for j in range(8):
                payload[d + j] = block[j * chunk : (j + 1) * chunk, :].astype(BF16)

        def send(k, carry):
            for copy in block_copies(lax.rem(me_t + k, n), me_t):
                copy.start()
            return carry

        lax.fori_loop(0, n, send, 0)
        down, up = halo_copies()

        @pl.when(me_t > 0)
        def _():
            down.wait_send()
            up.wait_recv()

        @pl.when(me_t < n - 1)
        def _():
            up.wait_send()
            down.wait_recv()

    @pl.when(step >= lead)
    def _():
        f = step - lead
        low_on = jnp.where(me_t > 0, 1.0, 0.0).astype(F32)
        high_on = jnp.where(me_t < n - 1, 1.0, 0.0).astype(F32)
        d = diff_ref[0, f]
        high, low = kron(vmix_ref, f, fields, levels)
        ext[:, PAD : PAD + tile_rows, :] = x_ref[0, 0]
        for r in range(2):
            ext[:, PAD - 2 + r : PAD - 1 + r, :] = (halo[0, f, r].astype(F32) * low_on)[:, None, :]
            at = PAD + tile_rows + r
            ext[:, at : at + 1, :] = (halo[1, f, r].astype(F32) * high_on)[:, None, :]
        total = tile_rows + 2 * PAD
        for g in range(total // GROUP):
            vert[g] = column(high, low, ext[:, g * GROUP : (g + 1) * GROUP, :], 3)
        row = iota((total, 1), 0)
        keep = jnp.where(row < PAD, low_on, jnp.where(row >= PAD + tile_rows, high_on, 1.0))
        for lev in range(levels):
            v = ext[lev]
            lift = vert[:, lev * GROUP : (lev + 1) * GROUP, :].reshape(total, width)
            out_ref[0, lev] = (v * (1.0 - 4.0 * d) + around(v) * d + lift) * keep

    @pl.when(step == pl.num_programs(0) - 1)
    def _():
        def finish(t, carry):
            for copy in block_copies(t, t):
                copy.wait()
            return carry

        lax.fori_loop(0, n, finish, 0)


def step_kernel(
    diff_ref,
    v_ref,
    vmix_ref,
    recv_ref,
    ids_ref,
    mask_ref,
    out_ref,
    vert,
    hits,
    packed,
):
    f = pl.program_id(0)
    n, chunk = recv_ref.shape[0], recv_ref.shape[1]
    levels, total, width = v_ref.shape[1], v_ref.shape[2], v_ref.shape[3]
    fields = vmix_ref.shape[2]
    rows = total - 2 * PAD
    xblocks = width // CELLS
    per_group = CELLS // LANE

    @pl.when(f == 0)
    def _():
        for g in range(n // per_group):
            ids = jnp.zeros((8, CELLS), F32)
            for j in range(per_group):
                ids = ids + ids_ref[g * per_group + j].astype(F32)
            ids = ids[0:1, :].astype(jnp.int32) - 1
            spot = jnp.where(ids >= 0, (ids % xblocks) * rows + ids // xblocks, -1)
            hits[:, g * CELLS : (g + 1) * CELLS] = onehot(
                iota((rows * xblocks, CELLS), 0) == spot, BF16
            )
        for t in range(n):
            packed[t, 0:chunk, :] = recv_ref[t]
            packed[t, chunk:, :] = jnp.zeros((LANE - chunk, packed.shape[2]), BF16)

    d = diff_ref[0, f]
    high, low = kron(vmix_ref, f, fields, levels)
    for g in range(rows // GROUP):
        at = PAD + g * GROUP
        vert[g] = column(high, low, v_ref[0, :, at : at + GROUP, :], 2)
    for lev in range(levels):
        v = v_ref[0, lev]
        lift = vert[:, lev * GROUP : (lev + 1) * GROUP, :].reshape(rows, width)
        near = v * (1.0 - 4.0 * d) + around(v) * d
        out_ref[0, 0, lev] = near[PAD : PAD + rows, :] + lift

    part = packed[:, :, pl.ds(pl.multiple_of(f * CELLS, CELLS), CELLS)].reshape(n * LANE, CELLS)
    forcing = jnp.dot(hits[...], part, preferred_element_type=F32)
    for xb in range(xblocks):
        cols = slice(xb * CELLS, (xb + 1) * CELLS)
        out_ref[0, 0, 0, :, cols] += forcing[xb * rows : (xb + 1) * rows, :] * mask_ref[
            0, :, cols
        ].astype(F32)


def local(
    model_state,
    sea_mask,
    diffusion,
    vertical_mix,
    export_mix,
    import_mix,
    pair_source,
    pair_tile,
    pair_block,
    pair_count,
    pair_weight,
):
    _, fields, levels, rows, width = model_state.shape
    channels = export_mix.shape[1]
    n = lax.axis_size("tile")
    slots = pair_source.shape[1]
    cap = (2 * slots + n - 1) // n
    chunk = -(-cap // 8) * 8
    wide = -(-slots // 128) * 128
    blocks = rows * width // CELLS
    total = rows + 2 * PAD
    lead = 4
    per_step = slots // lead
    last_rows = rows // 8 - 1

    vmix = vertical_mix.transpose(0, 2, 1, 3)
    smem = pl.BlockSpec(memory_space=pltpu.SMEM)
    hbm = pl.BlockSpec(memory_space=pl.ANY)

    def whole(shape):
        return pl.BlockSpec(shape, lambda i: (0,) * len(shape))

    def late(i):
        return lax.div(i, lead) * (i - lead)

    def early(i):
        return i + lax.div(i, lead) * (lead - 1 - i)

    received, ids, stepped = pl.pallas_call(
        functools.partial(send_kernel, cap, chunk, lead),
        grid=(lead + fields,),
        out_shape=(
            jax.ShapeDtypeStruct((n, chunk, fields * CELLS), BF16),
            jax.ShapeDtypeStruct((n, 8, CELLS), BF16),
            jax.ShapeDtypeStruct((fields, levels, total, width), F32),
        ),
        in_specs=[
            smem,
            smem,
            smem,
            whole((1, slots)),
            whole((1, slots)),
            whole((1, fields, 1, rows, width)),
            whole((1, fields, levels, 8, width)),
            pl.BlockSpec((1, fields, levels, 8, width), lambda i: (0, 0, 0, last_rows, 0)),
            whole((1, fields, channels)),
            whole((1, fields, channels)),
            whole((1, levels, fields, levels)),
            pl.BlockSpec((1, per_step, CELLS, CELLS), lambda i: (0, early(i), 0, 0)),
            pl.BlockSpec((1, 1, levels, rows, width), lambda i: (0, late(i), 0, 0, 0)),
        ],
        out_specs=(
            hbm,
            hbm,
            pl.BlockSpec((1, levels, total, width), lambda i: (late(i), 0, 0, 0)),
        ),
        scratch_shapes=[
            pltpu.VMEM((blocks, channels, CELLS), BF16),
            pltpu.VMEM((slots // GROUP, GROUP * channels, CELLS), BF16),
            pltpu.VMEM((wide, fields * CELLS), BF16),
            pltpu.VMEM((n, chunk, fields * CELLS), BF16),
            pltpu.VMEM((n, 8, CELLS), BF16),
            pltpu.VMEM((8, CELLS), F32),
            pltpu.VMEM((8, CELLS), F32),
            pltpu.VMEM((2, fields, 2, levels, width), BF16),
            pltpu.VMEM((2, fields, 2, levels, width), BF16),
            pltpu.VMEM((8, wide), jnp.int32),
            pltpu.VMEM((levels, total, width), F32),
            pltpu.VMEM((total // GROUP, levels * GROUP, width), F32),
            pltpu.SemaphoreType.DMA((n,)),
            pltpu.SemaphoreType.DMA((n,)),
            pltpu.SemaphoreType.DMA((n,)),
            pltpu.SemaphoreType.DMA((n,)),
            pltpu.SemaphoreType.DMA((3,)),
            pltpu.SemaphoreType.DMA((3,)),
        ],
        compiler_params=pltpu.CompilerParams(
            collective_id=0, has_side_effects=True, vmem_limit_bytes=58 << 20
        ),
    )(
        pair_source,
        pair_count,
        diffusion,
        pair_tile,
        pair_block,
        model_state,
        model_state,
        model_state,
        export_mix.transpose(0, 2, 1),
        import_mix,
        vmix,
        pair_weight,
        model_state,
    )

    return pl.pallas_call(
        step_kernel,
        grid=(fields,),
        out_shape=jax.ShapeDtypeStruct(model_state.shape, F32),
        in_specs=[
            smem,
            pl.BlockSpec((1, levels, total, width), lambda i: (i, 0, 0, 0)),
            whole((1, levels, fields, levels)),
            whole((n, chunk, fields * CELLS)),
            whole((n, 8, CELLS)),
            whole((1, rows, width)),
        ],
        out_specs=pl.BlockSpec((1, 1, levels, rows, width), lambda i: (0, i, 0, 0, 0)),
        scratch_shapes=[
            pltpu.VMEM((rows // GROUP, levels * GROUP, width), F32),
            pltpu.VMEM((blocks, n * LANE), BF16),
            pltpu.VMEM((n, LANE, fields * CELLS), BF16),
        ],
        compiler_params=pltpu.CompilerParams(vmem_limit_bytes=60 << 20),
    )(diffusion, stepped, vmix, received, ids, sea_mask)


def solution(mesh):
    return jax.shard_map(
        local,
        mesh=mesh,
        in_specs=(
            P("comp", None, None, "tile", None),
            P("comp", "tile", None),
            P("comp", None),
            P("comp", None, None, None),
            P("comp", None, None),
            P("comp", None, None),
            P("comp", "tile"),
            P("comp", "tile"),
            P("comp", "tile"),
            P("comp", "tile"),
            P("comp", "tile", None, None),
        ),
        out_specs=P("comp", None, None, "tile", None),
        check_vma=False,
    )
```
